32 devices in a mesh: tm: 4 (over y, core), space: 8 (over z, x).
Axes of the slice: x: 2, y: 2, z: 4, core: 2. Of those that a mesh axis runs over, the one named last changes fastest.
Arguments:
- initial: float32 [24, 192, 256], P('space'), may hold values from -1 to 1
- coarse_guess: float32 [4, 24, 192, 256], P('tm', 'space'), may hold values from -1 to 1
- react_rate: float32 [24, 192, 256], P('space'), may hold values from 0.5 to 3
Outputs:
- corrected: float32 [4, 24, 192, 256], P('tm', 'space')
- defect: float32 [4, 24, 192, 256], P('tm', 'space')
The draws below stay inside these ranges and needn't reach their ends.
All inputs are finite; a program needn't handle non-finite values.
Results may differ from the reference program's by a relative error of at most 0.00002.
Values sent between devices are 32-bit elements; how exact they have to be, the bound alone decides.
A program may use at most 64 MiB of HBM per device.

```python
import math
import jax
import jax.numpy as jnp
from jax import lax

NX = 192
NY = 256
STEPS = 3
NZ = 24
INTERVALS = 4


def levels(own_key, dims, cuts, smallest, largest):
    gain, own = 1.0, jax.random.fold_in(own_key, 6)
    for axis_at, parts in cuts:
        steps = jnp.exp(jax.random.uniform(jax.random.fold_in(own, axis_at), (parts,), jnp.float32, smallest / len(cuts), largest / len(cuts)))
        gain = gain * jnp.repeat(steps, dims[axis_at] // parts).reshape([-1 if axis == axis_at else 1 for axis in range(len(dims))])
    return gain


def setup_inputs(seed: int = 0) -> dict:
    key_of = jax.random.split(jax.random.key(seed), 4)
    initial = jnp.clip(jax.random.uniform(key_of[0], (NZ, NX, NY), jnp.float32, -1.0, 1.0) * levels(key_of[0], (NZ, NX, NY), ((0, 8),), -0.4, 0.0), -1.0, 1.0)
    coarse_guess = jnp.clip(jax.random.uniform(key_of[1], (INTERVALS, NZ, NX, NY), jnp.float32, -1.0, 1.0) * levels(key_of[1], (INTERVALS, NZ, NX, NY), ((0, 4), (1, 8)), -0.4, 0.0), -1.0, 1.0)
    react_rate = jnp.clip(jnp.exp(math.log(3.0) - 1.7917595 * jax.random.uniform(key_of[2], (NZ, NX, NY), jnp.float32) ** levels(key_of[2], (NZ, NX, NY), ((0, 8),), -0.2, 0.2)), 0.5, 3.0)
    return dict(initial=initial, coarse_guess=coarse_guess, react_rate=react_rate)


fine_diffuse = 0.04
fine_growth = 0.05
coarse_diffuse = 0.16
coarse_growth = 0.2


def explicit(current, react_rate, diffuse, growth):
    widths = [(0, 0)] * (current.ndim - 3) + [(1, 1)] * 3
    padded = jnp.pad(current, widths)
    beside = padded[..., 2:, 1:-1, 1:-1] + padded[..., :-2, 1:-1, 1:-1]
    beside = beside + padded[..., 1:-1, 2:, 1:-1] + padded[..., 1:-1, :-2, 1:-1]
    beside = beside + padded[..., 1:-1, 1:-1, 2:] + padded[..., 1:-1, 1:-1, :-2]
    return current + diffuse * (beside - 6.0 * current) + (growth * react_rate) * (current - current * current * current)


def reference(initial, coarse_guess, react_rate):
    starts = jnp.concatenate([initial[None], coarse_guess[:-1]], axis=0)
    current = starts
    for repeat in range(STEPS):
        current = explicit(current, react_rate, fine_diffuse, fine_growth)
    relaxed = current
    again = jnp.concatenate([initial[None], relaxed[:-1]], axis=0)
    current = again
    for repeat in range(STEPS):
        current = explicit(current, react_rate, fine_diffuse, fine_growth)
    fine_end = current
    defect = fine_end - relaxed
    offsets = fine_end - explicit(again, react_rate, coarse_diffuse, coarse_growth)

    def chain_turn(before, offset):
        after = explicit(before, react_rate, coarse_diffuse, coarse_growth) + offset
        return after, after

    unused, corrected = lax.scan(chain_turn, initial, offsets)
    return corrected, defect
```

```python
import functools

import jax
import jax.numpy as jnp
from jax import lax
from jax.experimental import pallas as pl
from jax.experimental.pallas import tpu as pltpu
from jax.sharding import PartitionSpec as P

STEPS = 3
SUBLANES = 8

fine_diffuse = 0.04
fine_growth = 0.05
coarse_ratio = 4.0

MESH = pl.DeviceIdType.MESH

START, RATE, AGAIN, CHAIN, DEFECT, CORRECTED = 0, 4, 8, 11, 14, 15
COPIES = 16


def kernel(
    nt, ns, planes, half, wide,
    initial, guess, rate_in, corrected_out, defect_out,
    start, rate, again, before, first, second, relaxed, coarse, offset, defect, after, reach,
    send, recv, local,
):
    tm, space = lax.axis_index("tm"), lax.axis_index("space")
    pair, side = lax.div(space, 2), lax.rem(space, 2)
    pairs = ns // 2
    mate = space + 1 - 2 * side
    block = 2 * planes
    length = block + 2 * STEPS
    rows = half + 2 * wide
    has_low, has_high = pair > 0, pair < pairs - 1
    has_next, has_previous = tm < nt - 1, tm > 0
    own = pl.ds(STEPS, block)

    for ref in (start, rate, again, before):
        zero_plane = jnp.zeros((STEPS,) + ref.shape[1:], jnp.float32)
        zero_rows = jnp.zeros((block, wide, ref.shape[2]), jnp.float32)
        ref[0:STEPS] = zero_plane
        ref[STEPS + block : length] = zero_plane
        ref[STEPS : STEPS + block, 0:wide] = zero_rows
        ref[STEPS : STEPS + block, wide + half : rows] = zero_rows

    barrier = pltpu.get_barrier_semaphore()
    count = jnp.int32(0)
    for step in (-1, 0, 1):
        for place in ("own", "mate", "low", "high"):
            if step == 0 and place == "own":
                continue
            there = {"own": space, "mate": mate, "low": space - 2, "high": space + 2}[place]
            tests = []
            if step:
                tests.append(has_next if step > 0 else has_previous)
            if place in ("low", "high"):
                tests.append(has_low if place == "low" else has_high)
            target = {"tm": tm + step, "space": there}
            if tests:
                valid = functools.reduce(jnp.logical_and, tests)

                @pl.when(valid)
                def _(target=target):
                    pl.semaphore_signal(barrier, inc=1, device_id=target, device_id_type=MESH)

                count = count + valid.astype(jnp.int32)
            else:
                pl.semaphore_signal(barrier, inc=1, device_id=target, device_id_type=MESH)
                count = count + 1
    pl.semaphore_wait(barrier, count)

    def remote(src, dst, slot, to_tm, to_space):
        return pltpu.make_async_remote_copy(
            src_ref=src,
            dst_ref=dst,
            send_sem=send.at[slot],
            recv_sem=recv.at[slot],
            device_id={"tm": to_tm, "space": to_space},
            device_id_type=MESH,
        )

    def cut(ref, target):
        return ref.at[:, pl.ds(pl.multiple_of(target * (half - wide), SUBLANES), half + wide), :]

    def spot(ref, target, begin, size):
        at = pl.multiple_of(wide * (1 - target), SUBLANES)
        return ref.at[pl.ds(begin, size), pl.ds(at, half + wide), :]

    slab = STEPS + planes * side
    other = STEPS + planes * (1 - side)

    rate_own = pltpu.make_async_copy(cut(rate_in, side), spot(rate, side, slab, planes), local.at[0])
    rate_mate = remote(
        cut(rate_in, 1 - side), spot(rate, 1 - side, slab, planes), RATE, tm, mate
    )
    initial_own = pltpu.make_async_copy(cut(initial, side), spot(start, side, slab, planes), local.at[1])
    initial_mate = remote(
        cut(initial, 1 - side), spot(start, 1 - side, slab, planes), START, tm, mate
    )
    guess_mate = remote(
        cut(guess, 1 - side), spot(start, 1 - side, slab, planes), START + 3, tm + 1, mate
    )
    guess_own = remote(
        cut(guess, side), spot(start, side, slab, planes), START + 2, tm + 1, space
    )

    @pl.when(tm == 0)
    def _():
        initial_mate.start()
        initial_own.start()

    @pl.when(has_next)
    def _():
        guess_mate.start()
        guess_own.start()

    rate_own.start()
    rate_mate.start()

    for ref in (first, second):
        @pl.when(jnp.logical_not(has_low))
        def _(ref=ref):
            ref[0:STEPS] = jnp.zeros((STEPS,) + ref.shape[1:], jnp.float32)

        @pl.when(jnp.logical_not(has_high))
        def _(ref=ref):
            ref[STEPS + block : length] = jnp.zeros((STEPS,) + ref.shape[1:], jnp.float32)

    row = lax.broadcasted_iota(jnp.int32, reach.shape, 0)
    outside = jnp.logical_or(
        jnp.logical_and(side == 0, row < wide), jnp.logical_and(side == 1, row >= wide + half)
    )
    reach[...] = jnp.where(outside, 0.0, fine_diffuse)

    def edges(ref, width, slot, to_tm):
        low = remote(
            spot(ref, side, STEPS, width), spot(ref, side, STEPS + block, width), slot, to_tm, space - 2
        )
        high = remote(
            spot(ref, side, STEPS + block - width, width),
            spot(ref, side, STEPS - width, width),
            slot + 1,
            to_tm,
            space + 2,
        )
        return low, high

    def send_edge(low, high, which):
        @pl.when(jnp.logical_and(which == 0, has_low))
        def _():
            low.start()

        @pl.when(jnp.logical_and(which == 1, has_high))
        def _():
            high.start()

    start_low, start_high = edges(start, STEPS, COPIES, tm)
    rate_low, rate_high = edges(rate, STEPS - 1, RATE + 1, tm)

    rate_own.wait()
    send_edge(rate_low, rate_high, side)

    @pl.when(tm == 0)
    def _():
        initial_own.wait()

    @pl.when(has_previous)
    def _():
        guess_own.wait_recv()

    send_edge(start_low, start_high, side)

    @pl.when(tm == 0)
    def _():
        initial_mate.wait_recv()

    @pl.when(has_previous)
    def _():
        guess_mate.wait_recv()

    send_edge(start_low, start_high, 1 - side)
    rate_mate.wait_recv()
    send_edge(rate_low, rate_high, 1 - side)

    @pl.when(has_high)
    def _():
        rate_low.wait_recv()
        start_low.wait_recv()

    @pl.when(has_low)
    def _():
        rate_high.wait_recv()
        start_high.wait_recv()

    keep = pltpu.make_async_copy(start, again, local.at[1])

    @pl.when(tm == 0)
    def _():
        keep.start()

    width = start.shape[2]
    lane = lax.broadcasted_iota(jnp.int32, reach.shape, 1)

    def change(ref, z):
        middle = ref[z]
        beside = ref[z + 1] + ref[z - 1]
        beside = beside + pltpu.roll(middle, 1, 0) + pltpu.roll(middle, rows - 1, 0)
        beside = beside + jnp.where(lane == 0, 0.0, pltpu.roll(middle, 1, 1))
        beside = beside + jnp.where(lane == width - 1, 0.0, pltpu.roll(middle, width - 1, 1))
        growth = rate[z] * (fine_growth - fine_growth * (middle * middle))
        return middle, reach[...] * beside + middle * (growth - 6.0 * fine_diffuse)

    def span(step):
        low = jnp.where(has_low, step, max(step, STEPS))
        high = jnp.where(has_high, length - step, min(length - step, STEPS + block))
        return low, high

    def fine(src, dst, step):
        def plane(z, carry):
            middle, delta = change(src, z)
            dst[z] = middle + delta
            return carry

        lax.fori_loop(*span(step), plane, 0)

    fine(start, first, 1)
    fine(first, second, 2)
    fine(second, relaxed, 3)

    def give(src, dst, width, slot):
        whole = remote(
            spot(src, side, STEPS, block), spot(dst, side, STEPS, block), slot, tm + 1, space
        )
        low = remote(
            spot(src, side, STEPS, width), spot(dst, side, STEPS + block, width), slot + 1, tm + 1, space - 2
        )
        high = remote(
            spot(src, side, STEPS + block - width, width),
            spot(dst, side, STEPS - width, width),
            slot + 2,
            tm + 1,
            space + 2,
        )
        return whole, low, high

    def begin(copies, valid):
        whole, low, high = copies
        pl.when(jnp.logical_and(valid, has_low))(low.start)
        pl.when(jnp.logical_and(valid, has_high))(high.start)
        pl.when(valid)(whole.start)

    def sent(copies, valid):
        whole, low, high = copies
        pl.when(jnp.logical_and(valid, has_low))(low.wait_send)
        pl.when(jnp.logical_and(valid, has_high))(high.wait_send)
        pl.when(valid)(whole.wait_send)

    def received(copies, valid):
        whole, low, high = copies
        pl.when(jnp.logical_and(valid, has_high))(low.wait_recv)
        pl.when(jnp.logical_and(valid, has_low))(high.wait_recv)
        pl.when(valid)(whole.wait_recv)

    given = give(relaxed, again, STEPS, AGAIN)
    begin(given, has_next)

    @pl.when(tm == 0)
    def _():
        keep.wait()

    received(given, has_previous)

    def first_plane(z, carry):
        middle, delta = change(again, z)
        first[z] = middle + delta
        coarse[z] = middle + coarse_ratio * delta
        return carry

    lax.fori_loop(*span(1), first_plane, 0)
    fine(first, second, 2)

    def last_plane(z, carry):
        middle, delta = change(second, z)
        end = middle + delta
        defect[z] = end - relaxed[z]
        shift = end - coarse[z]
        offset[z] = shift
        after[z] = coarse[z] + shift
        return carry

    lax.fori_loop(STEPS, STEPS + block, last_plane, 0)

    def back(src, dst, slot, lane_slot):
        mine = pl.ds(pl.multiple_of(side * half, SUBLANES), half)
        middle_rows = pl.ds(wide, half)
        stay = pltpu.make_async_copy(
            src.at[pl.ds(slab, planes), middle_rows, :], dst.at[:, mine, :], local.at[lane_slot]
        )
        go = remote(
            src.at[pl.ds(other, planes), middle_rows, :], dst.at[:, mine, :], slot, tm, mate
        )
        return stay, go

    defect_stay, defect_go = back(defect, defect_out, DEFECT, 2)

    passed = give(after, before, 1, CHAIN)
    later = tm > 1
    received(passed, later)

    @pl.when(later)
    def _():
        def plane(z, carry):
            middle, delta = change(before, z)
            after[z] = middle + coarse_ratio * delta + offset[z]
            return carry

        lax.fori_loop(STEPS, STEPS + block, plane, 0)

    onward = jnp.logical_and(tm > 0, has_next)
    begin(passed, onward)
    defect_go.start()
    defect_stay.start()
    corrected_stay, corrected_go = back(after, corrected_out, CORRECTED, 3)
    corrected_go.start()
    corrected_stay.start()

    @pl.when(tm == 0)
    def _():
        initial_mate.wait_send()

    @pl.when(has_next)
    def _():
        guess_own.wait_send()
        guess_mate.wait_send()

    rate_mate.wait_send()

    @pl.when(has_low)
    def _():
        rate_low.wait_send()
        start_low.wait_send()

    @pl.when(has_high)
    def _():
        rate_high.wait_send()
        start_high.wait_send()

    sent(given, has_next)
    sent(passed, onward)
    defect_stay.wait()
    corrected_stay.wait()
    defect_go.wait()
    corrected_go.wait()


def on_device(nt, ns, initial, coarse_guess, react_rate):
    planes, across, width = initial.shape
    half = across // 2
    wide = -(-(2 * STEPS + max(nt - 2, 0)) // SUBLANES) * SUBLANES
    length = 2 * planes + 2 * STEPS
    field = pltpu.VMEM((length, half + 2 * wide, width), jnp.float32)
    shape = jax.ShapeDtypeStruct(initial.shape, jnp.float32)
    corrected, defect = pl.pallas_call(
        functools.partial(kernel, nt, ns, planes, half, wide),
        out_shape=(shape, shape),
        in_specs=[pl.BlockSpec(memory_space=pl.ANY)] * 3,
        out_specs=[pl.BlockSpec(memory_space=pl.ANY)] * 2,
        scratch_shapes=[field] * 11
        + [
            pltpu.VMEM((half + 2 * wide, width), jnp.float32),
            pltpu.SemaphoreType.DMA((COPIES + 2,)),
            pltpu.SemaphoreType.DMA((COPIES + 2,)),
            pltpu.SemaphoreType.DMA((4,)),
        ],
        compiler_params=pltpu.CompilerParams(collective_id=0, has_side_effects=True),
    )(initial, coarse_guess[0], react_rate)
    return corrected[None], defect[None]


def solution(mesh):
    in_specs = (P("space", None, None), P("tm", "space", None, None), P("space", None, None))
    out_specs = (P("tm", "space", None, None), P("tm", "space", None, None))
    return jax.shard_map(
        functools.partial(on_device, mesh.shape["tm"], mesh.shape["space"]),
        mesh=mesh, in_specs=in_specs, out_specs=out_specs, check_vma=False,
    )
```

```python
import functools

import jax
import jax.numpy as jnp
from jax import lax
from jax.experimental import pallas as pl
from jax.experimental.pallas import tpu as pltpu
from jax.sharding import PartitionSpec as P

STEPS = 3
SUBLANES = 8

fine_diffuse = 0.04
fine_growth = 0.05
coarse_ratio = 4.0

MESH = pl.DeviceIdType.MESH

PIECES = 4


def slots(planes):
    kinds = dict(
        start=4, start_edge=2, rate=1, rate_edge=2, again=PIECES, again_edge=2 * PIECES,
        chain=2 * planes, chain_edge=2, defect=1, corrected=planes,
    )
    first, total = {}, 0
    for kind, number in kinds.items():
        first[kind] = total
        total += number
    return first, total


def kernel(
    nt, ns, planes, half, wide, slot_of,
    initial, guess, rate_in, corrected_out, defect_out,
    start, rate, again, before, first, second, relaxed, coarse, offset, defect, after, reach,
    send, recv, local,
):
    tm, space = lax.axis_index("tm"), lax.axis_index("space")
    pair, side = lax.div(space, 2), lax.rem(space, 2)
    pairs = ns // 2
    mate = space + 1 - 2 * side
    block = 2 * planes
    length = block + 2 * STEPS
    rows = half + 2 * wide
    has_low, has_high = pair > 0, pair < pairs - 1
    has_next, has_previous = tm < nt - 1, tm > 0
    own = pl.ds(STEPS, block)

    for ref in (start, rate, again, before):
        zero_plane = jnp.zeros((STEPS,) + ref.shape[1:], jnp.float32)
        zero_rows = jnp.zeros((block, wide, ref.shape[2]), jnp.float32)
        ref[0:STEPS] = zero_plane
        ref[STEPS + block : length] = zero_plane
        ref[STEPS : STEPS + block, 0:wide] = zero_rows
        ref[STEPS : STEPS + block, wide + half : rows] = zero_rows

    barrier = pltpu.get_barrier_semaphore()
    count = jnp.int32(0)
    for step in (-1, 0, 1):
        for place in ("own", "mate", "low", "high"):
            if step == 0 and place == "own":
                continue
            there = {"own": space, "mate": mate, "low": space - 2, "high": space + 2}[place]
            tests = []
            if step:
                tests.append(has_next if step > 0 else has_previous)
            if place in ("low", "high"):
                tests.append(has_low if place == "low" else has_high)
            target = {"tm": tm + step, "space": there}
            if tests:
                valid = functools.reduce(jnp.logical_and, tests)

                @pl.when(valid)
                def _(target=target):
                    pl.semaphore_signal(barrier, inc=1, device_id=target, device_id_type=MESH)

                count = count + valid.astype(jnp.int32)
            else:
                pl.semaphore_signal(barrier, inc=1, device_id=target, device_id_type=MESH)
                count = count + 1
    pl.semaphore_wait(barrier, count)

    def remote(src, dst, slot, to_tm, to_space):
        return pltpu.make_async_remote_copy(
            src_ref=src,
            dst_ref=dst,
            send_sem=send.at[slot],
            recv_sem=recv.at[slot],
            device_id={"tm": to_tm, "space": to_space},
            device_id_type=MESH,
        )

    def cut(ref, target):
        return ref.at[:, pl.ds(pl.multiple_of(target * (half - wide), SUBLANES), half + wide), :]

    def spot(ref, target, begin, size):
        at = pl.multiple_of(wide * (1 - target), SUBLANES)
        return ref.at[pl.ds(begin, size), pl.ds(at, half + wide), :]

    slab = STEPS + planes * side
    other = STEPS + planes * (1 - side)

    rate_own = pltpu.make_async_copy(cut(rate_in, side), spot(rate, side, slab, planes), local.at[0])
    rate_mate = remote(
        cut(rate_in, 1 - side), spot(rate, 1 - side, slab, planes), slot_of["rate"], tm, mate
    )
    initial_own = pltpu.make_async_copy(cut(initial, side), spot(start, side, slab, planes), local.at[1])
    initial_mate = remote(
        cut(initial, 1 - side), spot(start, 1 - side, slab, planes), slot_of["start"], tm, mate
    )
    guess_mate = remote(
        cut(guess, 1 - side), spot(start, 1 - side, slab, planes), slot_of["start"] + 3, tm + 1, mate
    )
    guess_own = remote(
        cut(guess, side), spot(start, side, slab, planes), slot_of["start"] + 2, tm + 1, space
    )

    @pl.when(tm == 0)
    def _():
        initial_mate.start()
        initial_own.start()

    @pl.when(has_next)
    def _():
        guess_mate.start()
        guess_own.start()

    rate_own.start()
    rate_mate.start()

    for ref in (first, second):
        @pl.when(jnp.logical_not(has_low))
        def _(ref=ref):
            ref[0:STEPS] = jnp.zeros((STEPS,) + ref.shape[1:], jnp.float32)

        @pl.when(jnp.logical_not(has_high))
        def _(ref=ref):
            ref[STEPS + block : length] = jnp.zeros((STEPS,) + ref.shape[1:], jnp.float32)

    row = lax.broadcasted_iota(jnp.int32, reach.shape, 0)
    outside = jnp.logical_or(
        jnp.logical_and(side == 0, row < wide), jnp.logical_and(side == 1, row >= wide + half)
    )
    reach[...] = jnp.where(outside, 0.0, fine_diffuse)

    def edges(ref, width, slot, to_tm):
        low = remote(
            spot(ref, side, STEPS, width), spot(ref, side, STEPS + block, width), slot, to_tm, space - 2
        )
        high = remote(
            spot(ref, side, STEPS + block - width, width),
            spot(ref, side, STEPS - width, width),
            slot + 1,
            to_tm,
            space + 2,
        )
        return low, high

    def send_edge(low, high, which):
        @pl.when(jnp.logical_and(which == 0, has_low))
        def _():
            low.start()

        @pl.when(jnp.logical_and(which == 1, has_high))
        def _():
            high.start()

    start_low, start_high = edges(start, STEPS, slot_of["start_edge"], tm)
    rate_low, rate_high = edges(rate, STEPS - 1, slot_of["rate_edge"], tm)

    rate_own.wait()
    send_edge(rate_low, rate_high, side)

    @pl.when(tm == 0)
    def _():
        initial_own.wait()

    @pl.when(has_previous)
    def _():
        guess_own.wait_recv()

    send_edge(start_low, start_high, side)

    @pl.when(tm == 0)
    def _():
        initial_mate.wait_recv()

    @pl.when(has_previous)
    def _():
        guess_mate.wait_recv()

    send_edge(start_low, start_high, 1 - side)
    rate_mate.wait_recv()
    send_edge(rate_low, rate_high, 1 - side)

    @pl.when(has_high)
    def _():
        rate_low.wait_recv()
        start_low.wait_recv()

    @pl.when(has_low)
    def _():
        rate_high.wait_recv()
        start_high.wait_recv()

    keep = pltpu.make_async_copy(start, again, local.at[1])

    @pl.when(tm == 0)
    def _():
        keep.start()

    width = start.shape[2]
    lane = lax.broadcasted_iota(jnp.int32, reach.shape, 1)

    def change(ref, z):
        middle = ref[z]
        beside = ref[z + 1] + ref[z - 1]
        beside = beside + pltpu.roll(middle, 1, 0) + pltpu.roll(middle, rows - 1, 0)
        beside = beside + jnp.where(lane == 0, 0.0, pltpu.roll(middle, 1, 1))
        beside = beside + jnp.where(lane == width - 1, 0.0, pltpu.roll(middle, width - 1, 1))
        growth = rate[z] * (fine_growth - fine_growth * (middle * middle))
        return middle, reach[...] * beside + middle * (growth - 6.0 * fine_diffuse)

    def span(step):
        low = jnp.where(has_low, step, max(step, STEPS))
        high = jnp.where(has_high, length - step, min(length - step, STEPS + block))
        return low, high

    def fine(src, dst, step):
        def plane(z, carry):
            middle, delta = change(src, z)
            dst[z] = middle + delta
            return carry

        lax.fori_loop(*span(step), plane, 0)

    fine(start, first, 1)
    fine(first, second, 2)
    fine(second, relaxed, 3)

    groups = (half + wide) // SUBLANES
    bounds = [groups * piece // PIECES * SUBLANES for piece in range(PIECES + 1)]

    def piece_of(ref, begin, size, piece):
        at = pl.multiple_of(wide * (1 - side) + bounds[piece], SUBLANES)
        return ref.at[pl.ds(begin, size), pl.ds(at, bounds[piece + 1] - bounds[piece]), :]

    given, given_low, given_high = [], [], []
    for piece in range(PIECES):
        slot = slot_of["again_edge"] + 2 * piece
        given.append(
            remote(
                piece_of(relaxed, STEPS, block, piece),
                piece_of(again, STEPS, block, piece),
                slot_of["again"] + piece,
                tm + 1,
                space,
            )
        )
        given_low.append(
            remote(
                piece_of(again, STEPS, STEPS, piece),
                piece_of(again, STEPS + block, STEPS, piece),
                slot,
                tm,
                space - 2,
            )
        )
        given_high.append(
            remote(
                piece_of(again, block, STEPS, piece),
                piece_of(again, 0, STEPS, piece),
                slot + 1,
                tm,
                space + 2,
            )
        )

    @pl.when(has_next)
    def _():
        for piece in range(PIECES):
            given[piece].start()

    @pl.when(tm == 0)
    def _():
        keep.wait()

    @pl.when(has_previous)
    def _():
        for piece in range(PIECES):
            given[piece].wait_recv()
            pl.when(has_low)(given_low[piece].start)
            pl.when(has_high)(given_high[piece].start)
        for piece in range(PIECES):
            pl.when(has_high)(given_low[piece].wait_recv)
            pl.when(has_low)(given_high[piece].wait_recv)

    def first_plane(z, carry):
        middle, delta = change(again, z)
        first[z] = middle + delta
        coarse[z] = middle + coarse_ratio * delta
        return carry

    lax.fori_loop(*span(1), first_plane, 0)
    fine(first, second, 2)

    order = []
    for depth in range(planes):
        order += [STEPS + depth, STEPS + block - 1 - depth]

    def row_span(z):
        at = pl.multiple_of(wide * (1 - side), SUBLANES)
        return (pl.ds(z, 1), pl.ds(at, half + wide), slice(None))

    passed = {
        z: remote(
            after.at[row_span(z)], before.at[row_span(z)], slot_of["chain"] + z - STEPS, tm + 1, space
        )
        for z in order
    }
    low_edge, high_edge = STEPS, STEPS + block - 1
    passed_low = remote(
        before.at[row_span(low_edge)], before.at[row_span(high_edge + 1)],
        slot_of["chain_edge"], tm, space - 2,
    )
    passed_high = remote(
        before.at[row_span(high_edge)], before.at[row_span(low_edge - 1)],
        slot_of["chain_edge"] + 1, tm, space + 2,
    )

    mine = pl.ds(pl.multiple_of(side * half, SUBLANES), half)
    middle_rows = pl.ds(wide, half)
    defect_stay = pltpu.make_async_copy(
        defect.at[pl.ds(slab, planes), middle_rows, :], defect_out.at[:, mine, :], local.at[2]
    )
    defect_go = remote(
        defect.at[pl.ds(other, planes), middle_rows, :], defect_out.at[:, mine, :],
        slot_of["defect"], tm, mate,
    )
    stay, go = {}, {}
    for z in order:
        place = (z - STEPS) % planes
        src = after.at[pl.ds(z, 1), middle_rows, :]
        dst = corrected_out.at[pl.ds(place, 1), mine, :]
        stay[z] = pltpu.make_async_copy(src, dst, local.at[3 + place])
        go[z] = remote(src, dst, slot_of["corrected"] + place, tm, mate)

    def at_home(z):
        return side == (z - STEPS) // planes

    def hand_in(z):
        pl.when(at_home(z))(stay[z].start)
        pl.when(jnp.logical_not(at_home(z)))(go[z].start)

    def last_plane(z):
        middle, delta = change(second, z)
        end = middle + delta
        defect[z] = end - relaxed[z]
        shift = end - coarse[z]
        offset[z] = shift
        after[z] = coarse[z] + shift

    opens = jnp.logical_and(tm == 1, has_next)
    for index, z in enumerate(order):
        last_plane(z)
        if index:
            pl.when(opens)(passed[order[index - 1]].start)
    pl.when(opens)(passed[order[-1]].start)
    defect_go.start()
    defect_stay.start()

    later = tm > 1

    @pl.when(jnp.logical_not(later))
    def _():
        for z in order:
            hand_in(z)

    @pl.when(later)
    def _():
        queue = list(order)
        waiting = set(order)

        def leave(z):
            pl.when(has_next)(passed[z].start)
            hand_in(z)

        for index, z in enumerate(order):
            while waiting & {z - 1, z, z + 1}:
                come = queue.pop(0)
                waiting.remove(come)
                passed[come].wait_recv()
                if come == low_edge:
                    pl.when(has_low)(passed_low.start)
                if come == high_edge:
                    pl.when(has_high)(passed_high.start)
            if z == low_edge:
                pl.when(has_low)(passed_high.wait_recv)
            if z == high_edge:
                pl.when(has_high)(passed_low.wait_recv)
            middle, delta = change(before, z)
            after[z] = middle + coarse_ratio * delta + offset[z]
            if index:
                leave(order[index - 1])
        leave(order[-1])
        pl.when(has_low)(passed_low.wait_send)
        pl.when(has_high)(passed_high.wait_send)

    onward = jnp.logical_and(tm > 0, has_next)

    @pl.when(tm == 0)
    def _():
        initial_mate.wait_send()

    @pl.when(has_next)
    def _():
        guess_own.wait_send()
        guess_mate.wait_send()

    rate_mate.wait_send()

    @pl.when(has_low)
    def _():
        rate_low.wait_send()
        start_low.wait_send()

    @pl.when(has_high)
    def _():
        rate_high.wait_send()
        start_high.wait_send()

    @pl.when(has_next)
    def _():
        for piece in range(PIECES):
            given[piece].wait_send()

    @pl.when(has_previous)
    def _():
        for piece in range(PIECES):
            pl.when(has_low)(given_low[piece].wait_send)
            pl.when(has_high)(given_high[piece].wait_send)

    @pl.when(onward)
    def _():
        for z in order:
            passed[z].wait_send()

    defect_stay.wait()
    defect_go.wait()
    for z in order:
        pl.when(at_home(z))(stay[z].wait)
        pl.when(at_home(z))(go[z].wait_recv)
        pl.when(jnp.logical_not(at_home(z)))(go[z].wait_send)


def on_device(nt, ns, initial, coarse_guess, react_rate):
    planes, across, width = initial.shape
    half = across // 2
    wide = -(-(2 * STEPS + max(nt - 2, 0)) // SUBLANES) * SUBLANES
    length = 2 * planes + 2 * STEPS
    field = pltpu.VMEM((length, half + 2 * wide, width), jnp.float32)
    slot_of, total = slots(planes)
    shape = jax.ShapeDtypeStruct(initial.shape, jnp.float32)
    corrected, defect = pl.pallas_call(
        functools.partial(kernel, nt, ns, planes, half, wide, slot_of),
        out_shape=(shape, shape),
        in_specs=[pl.BlockSpec(memory_space=pl.ANY)] * 3,
        out_specs=[pl.BlockSpec(memory_space=pl.ANY)] * 2,
        scratch_shapes=[field] * 11
        + [
            pltpu.VMEM((half + 2 * wide, width), jnp.float32),
            pltpu.SemaphoreType.DMA((total,)),
            pltpu.SemaphoreType.DMA((total,)),
            pltpu.SemaphoreType.DMA((3 + planes,)),
        ],
        compiler_params=pltpu.CompilerParams(collective_id=0, has_side_effects=True),
    )(initial, coarse_guess[0], react_rate)
    return corrected[None], defect[None]


def solution(mesh):
    in_specs = (P("space", None, None), P("tm", "space", None, None), P("space", None, None))
    out_specs = (P("tm", "space", None, None), P("tm", "space", None, None))
    return jax.shard_map(
        functools.partial(on_device, mesh.shape["tm"], mesh.shape["space"]),
        mesh=mesh, in_specs=in_specs, out_specs=out_specs, check_vma=False,
    )
```

```python
import functools

import jax
import jax.numpy as jnp
from jax import lax
from jax.experimental import pallas as pl
from jax.experimental.pallas import tpu as pltpu
from jax.sharding import PartitionSpec as P

STEPS = 3
SUBLANES = 8

fine_diffuse = 0.04
fine_growth = 0.05
coarse_ratio = 4.0

MESH = pl.DeviceIdType.MESH

PIECES = 4


def slots(planes):
    kinds = dict(
        start=2 + PIECES, start_edge=1 + PIECES, rate=1, rate_edge=2, rate_core=3, again=PIECES, again_edge=2 * PIECES,
        chain=2 * planes, chain_edge=2, defect=1, corrected=planes,
    )
    first, total = {}, 0
    for kind, number in kinds.items():
        first[kind] = total
        total += number
    return first, total


def kernel(
    nt, ns, planes, half, wide, slot_of,
    initial, guess, rate_in, corrected_out, defect_out,
    start, rate, again, before, first, second, relaxed, coarse, offset, defect, after, reach,
    send, recv, local,
):
    tm, space = lax.axis_index("tm"), lax.axis_index("space")
    pair, side = lax.div(space, 2), lax.rem(space, 2)
    pairs = ns // 2
    mate = space + 1 - 2 * side
    block = 2 * planes
    length = block + 2 * STEPS
    rows = half + 2 * wide
    has_low, has_high = pair > 0, pair < pairs - 1
    has_next, has_previous = tm < nt - 1, tm > 0
    own = pl.ds(STEPS, block)

    for ref in (start, rate, again, before):
        zero_plane = jnp.zeros((STEPS,) + ref.shape[1:], jnp.float32)
        zero_rows = jnp.zeros((block, wide, ref.shape[2]), jnp.float32)
        ref[0:STEPS] = zero_plane
        ref[STEPS + block : length] = zero_plane
        ref[STEPS : STEPS + block, 0:wide] = zero_rows
        ref[STEPS : STEPS + block, wide + half : rows] = zero_rows

    barrier = pltpu.get_barrier_semaphore()
    count = jnp.int32(0)
    for step in (-1, 0, 1):
        for place in ("own", "mate", "low", "high"):
            if step == 0 and place == "own":
                continue
            there = {"own": space, "mate": mate, "low": space - 2, "high": space + 2}[place]
            tests = []
            if step:
                tests.append(has_next if step > 0 else has_previous)
            if place in ("low", "high"):
                tests.append(has_low if place == "low" else has_high)
            target = {"tm": tm + step, "space": there}
            if tests:
                valid = functools.reduce(jnp.logical_and, tests)

                @pl.when(valid)
                def _(target=target):
                    pl.semaphore_signal(barrier, inc=1, device_id=target, device_id_type=MESH)

                count = count + valid.astype(jnp.int32)
            else:
                pl.semaphore_signal(barrier, inc=1, device_id=target, device_id_type=MESH)
                count = count + 1
    for here, there in ((tm == 0, nt - 1), (tm == nt - 1, 0)):

        @pl.when(here)
        def _(there=there):
            pl.semaphore_signal(
                barrier, inc=1, device_id={"tm": there, "space": mate}, device_id_type=MESH
            )

        count = count + here.astype(jnp.int32)
    pl.semaphore_wait(barrier, count)

    def remote(src, dst, slot, to_tm, to_space):
        return pltpu.make_async_remote_copy(
            src_ref=src,
            dst_ref=dst,
            send_sem=send.at[slot],
            recv_sem=recv.at[slot],
            device_id={"tm": to_tm, "space": to_space},
            device_id_type=MESH,
        )

    def cut(ref, target):
        return ref.at[:, pl.ds(pl.multiple_of(target * (half - wide), SUBLANES), half + wide), :]

    def spot(ref, target, begin, size):
        at = pl.multiple_of(wide * (1 - target), SUBLANES)
        return ref.at[pl.ds(begin, size), pl.ds(at, half + wide), :]

    slab = STEPS + planes * side
    other = STEPS + planes * (1 - side)

    core = lax.rem(tm, 2)
    twin = tm + 1 - 2 * core
    lanes = start.shape[2] // 2

    def lane_half(ref, which):
        return ref.at[:, :, pl.ds(pl.multiple_of(which * lanes, lanes), lanes)]

    groups = (half + wide) // SUBLANES
    bounds = [groups * piece // PIECES * SUBLANES for piece in range(PIECES + 1)]

    def piece_of(ref, begin, size, piece, target=side):
        at = pl.multiple_of(wide * (1 - target) + bounds[piece], SUBLANES)
        return ref.at[pl.ds(begin, size), pl.ds(at, bounds[piece + 1] - bounds[piece]), :]

    def cut_piece(ref, target, piece):
        at = pl.multiple_of(target * (half - wide) + bounds[piece], SUBLANES)
        return ref.at[:, pl.ds(at, bounds[piece + 1] - bounds[piece]), :]

    rate_own = pltpu.make_async_copy(cut(rate_in, side), spot(rate, side, slab, planes), local.at[0])
    rate_mate = remote(
        lane_half(cut(rate_in, 1 - side), core),
        lane_half(spot(rate, 1 - side, slab, planes), core),
        slot_of["rate"],
        tm,
        mate,
    )
    initial_own = pltpu.make_async_copy(cut(initial, side), spot(start, side, slab, planes), local.at[1])
    guess_own = remote(
        cut(guess, side), spot(start, side, slab, planes), slot_of["start"], tm + 1, space
    )

    def to_mate(ref, to_tm):
        return [
            remote(
                cut_piece(ref, 1 - side, piece),
                piece_of(start, slab, planes, piece, 1 - side),
                slot_of["start"] + 1 + piece,
                to_tm,
                mate,
            )
            for piece in range(PIECES)
        ]

    guess_mate = to_mate(guess, tm + 1)
    initial_mate = to_mate(initial, 0)
    is_last = tm == nt - 1

    rate_mate.start()
    rate_own.start()

    @pl.when(has_next)
    def _():
        guess_own.start()
        for copy in guess_mate:
            copy.start()

    @pl.when(is_last)
    def _():
        for copy in initial_mate:
            copy.start()

    @pl.when(tm == 0)
    def _():
        initial_own.start()

    for ref in (first, second):
        @pl.when(jnp.logical_not(has_low))
        def _(ref=ref):
            ref[0:STEPS] = jnp.zeros((STEPS,) + ref.shape[1:], jnp.float32)

        @pl.when(jnp.logical_not(has_high))
        def _(ref=ref):
            ref[STEPS + block : length] = jnp.zeros((STEPS,) + ref.shape[1:], jnp.float32)

    row = lax.broadcasted_iota(jnp.int32, reach.shape, 0)
    outside = jnp.logical_or(
        jnp.logical_and(side == 0, row < wide), jnp.logical_and(side == 1, row >= wide + half)
    )
    reach[...] = jnp.where(outside, 0.0, fine_diffuse)

    low_place, high_place = STEPS + block, 0

    def edge_pieces(piece):
        slot = slot_of["start_edge"] + 1 + piece
        low = remote(
            piece_of(start, STEPS, STEPS, piece), piece_of(start, low_place, STEPS, piece),
            slot, tm, space - 2,
        )
        high = remote(
            piece_of(start, block, STEPS, piece), piece_of(start, high_place, STEPS, piece),
            slot, tm, space + 2,
        )
        return low, high

    start_edges = [edge_pieces(piece) for piece in range(PIECES)]
    start_low = remote(
        spot(start, side, STEPS, STEPS), spot(start, side, low_place, STEPS),
        slot_of["start_edge"], tm, space - 2,
    )
    start_high = remote(
        spot(start, side, block, STEPS), spot(start, side, high_place, STEPS),
        slot_of["start_edge"], tm, space + 2,
    )
    reach_rate = STEPS - 1
    rate_low_spot = lane_half(spot(rate, side, low_place, reach_rate), core)
    rate_high_spot = lane_half(spot(rate, side, high_place + 1, reach_rate), core)
    rate_low = remote(
        lane_half(spot(rate, side, STEPS, reach_rate), core), rate_low_spot,
        slot_of["rate_edge"], tm, space - 2,
    )
    rate_high = remote(
        lane_half(spot(rate, side, STEPS + block - reach_rate, reach_rate), core), rate_high_spot,
        slot_of["rate_edge"] + 1, tm, space + 2,
    )
    rate_other_spot = lane_half(spot(rate, side, other, planes), core)
    twin_mate = remote(rate_other_spot, rate_other_spot, slot_of["rate_core"], twin, space)
    twin_low = remote(rate_low_spot, rate_low_spot, slot_of["rate_core"] + 1, twin, space)
    twin_high = remote(rate_high_spot, rate_high_spot, slot_of["rate_core"] + 2, twin, space)

    own_low = jnp.logical_and(side == 0, has_low)
    own_high = jnp.logical_and(side == 1, has_high)
    other_low = jnp.logical_and(side == 1, has_low)
    other_high = jnp.logical_and(side == 0, has_high)

    rate_own.wait()
    pl.when(own_low)(rate_low.start)
    pl.when(own_high)(rate_high.start)

    @pl.when(tm == 0)
    def _():
        initial_own.wait()

    @pl.when(has_previous)
    def _():
        guess_own.wait_recv()

    pl.when(own_low)(start_low.start)
    pl.when(own_high)(start_high.start)

    rate_mate.wait_recv()
    pl.when(other_low)(rate_low.start)
    pl.when(other_high)(rate_high.start)
    twin_mate.start()

    for piece in range(PIECES):
        guess_mate[piece].wait_recv()
        pl.when(other_low)(start_edges[piece][0].start)
        pl.when(other_high)(start_edges[piece][1].start)

    @pl.when(has_high)
    def _():
        rate_low.wait_recv()
        twin_low.start()

    @pl.when(has_low)
    def _():
        rate_high.wait_recv()
        twin_high.start()

    twin_mate.wait_recv()
    pl.when(has_high)(twin_low.wait_recv)
    pl.when(has_low)(twin_high.wait_recv)

    @pl.when(jnp.logical_and(side == 0, has_high))
    def _():
        start_low.wait_recv()

    @pl.when(jnp.logical_and(side == 1, has_low))
    def _():
        start_high.wait_recv()

    @pl.when(jnp.logical_and(side == 1, has_high))
    def _():
        for low, high in start_edges:
            low.wait_recv()

    @pl.when(jnp.logical_and(side == 0, has_low))
    def _():
        for low, high in start_edges:
            high.wait_recv()

    keep = pltpu.make_async_copy(start, again, local.at[1])

    @pl.when(tm == 0)
    def _():
        keep.start()

    width = start.shape[2]
    lane = lax.broadcasted_iota(jnp.int32, reach.shape, 1)

    def change(ref, z):
        middle = ref[z]
        beside = ref[z + 1] + ref[z - 1]
        beside = beside + pltpu.roll(middle, 1, 0) + pltpu.roll(middle, rows - 1, 0)
        beside = beside + jnp.where(lane == 0, 0.0, pltpu.roll(middle, 1, 1))
        beside = beside + jnp.where(lane == width - 1, 0.0, pltpu.roll(middle, width - 1, 1))
        growth = rate[z] * (fine_growth - fine_growth * (middle * middle))
        return middle, reach[...] * beside + middle * (growth - 6.0 * fine_diffuse)

    def span(step):
        low = jnp.where(has_low, step, max(step, STEPS))
        high = jnp.where(has_high, length - step, min(length - step, STEPS + block))
        return low, high

    def fine(src, dst, step):
        def plane(z, carry):
            middle, delta = change(src, z)
            dst[z] = middle + delta
            return carry

        lax.fori_loop(*span(step), plane, 0)

    fine(start, first, 1)
    fine(first, second, 2)
    fine(second, relaxed, 3)

    given, given_low, given_high = [], [], []
    for piece in range(PIECES):
        slot = slot_of["again_edge"] + 2 * piece
        given.append(
            remote(
                piece_of(relaxed, STEPS, block, piece),
                piece_of(again, STEPS, block, piece),
                slot_of["again"] + piece,
                tm + 1,
                space,
            )
        )
        given_low.append(
            remote(
                piece_of(again, STEPS, STEPS, piece),
                piece_of(again, STEPS + block, STEPS, piece),
                slot,
                tm,
                space - 2,
            )
        )
        given_high.append(
            remote(
                piece_of(again, block, STEPS, piece),
                piece_of(again, 0, STEPS, piece),
                slot + 1,
                tm,
                space + 2,
            )
        )

    @pl.when(has_next)
    def _():
        for piece in range(PIECES):
            given[piece].start()

    @pl.when(tm == 0)
    def _():
        keep.wait()

    @pl.when(has_previous)
    def _():
        for piece in range(PIECES):
            given[piece].wait_recv()
            pl.when(has_low)(given_low[piece].start)
            pl.when(has_high)(given_high[piece].start)
        for piece in range(PIECES):
            pl.when(has_high)(given_low[piece].wait_recv)
            pl.when(has_low)(given_high[piece].wait_recv)

    def first_plane(z, carry):
        middle, delta = change(again, z)
        first[z] = middle + delta
        coarse[z] = middle + coarse_ratio * delta
        return carry

    lax.fori_loop(*span(1), first_plane, 0)
    fine(first, second, 2)

    order = []
    for depth in range(planes):
        order += [STEPS + depth, STEPS + block - 1 - depth]

    def row_span(z):
        at = pl.multiple_of(wide * (1 - side), SUBLANES)
        return (pl.ds(z, 1), pl.ds(at, half + wide), slice(None))

    passed = {
        z: remote(
            after.at[row_span(z)], before.at[row_span(z)], slot_of["chain"] + z - STEPS, tm + 1, space
        )
        for z in order
    }
    low_edge, high_edge = STEPS, STEPS + block - 1
    passed_low = remote(
        before.at[row_span(low_edge)], before.at[row_span(high_edge + 1)],
        slot_of["chain_edge"], tm, space - 2,
    )
    passed_high = remote(
        before.at[row_span(high_edge)], before.at[row_span(low_edge - 1)],
        slot_of["chain_edge"] + 1, tm, space + 2,
    )

    mine = pl.ds(pl.multiple_of(side * half, SUBLANES), half)
    middle_rows = pl.ds(wide, half)
    defect_stay = pltpu.make_async_copy(
        defect.at[pl.ds(slab, planes), middle_rows, :], defect_out.at[:, mine, :], local.at[2]
    )
    defect_go = remote(
        defect.at[pl.ds(other, planes), middle_rows, :], defect_out.at[:, mine, :],
        slot_of["defect"], tm, mate,
    )
    stay, go = {}, {}
    for z in order:
        place = (z - STEPS) % planes
        src = after.at[pl.ds(z, 1), middle_rows, :]
        dst = corrected_out.at[pl.ds(place, 1), mine, :]
        stay[z] = pltpu.make_async_copy(src, dst, local.at[3 + place])
        go[z] = remote(src, dst, slot_of["corrected"] + place, tm, mate)

    def at_home(z):
        return side == (z - STEPS) // planes

    def hand_in(z):
        pl.when(at_home(z))(stay[z].start)
        pl.when(jnp.logical_not(at_home(z)))(go[z].start)

    def last_plane(z):
        middle, delta = change(second, z)
        end = middle + delta
        defect[z] = end - relaxed[z]
        shift = end - coarse[z]
        offset[z] = shift
        after[z] = coarse[z] + shift

    opens = jnp.logical_and(tm == 1, has_next)
    for index, z in enumerate(order):
        last_plane(z)
        if index:
            pl.when(opens)(passed[order[index - 1]].start)
    pl.when(opens)(passed[order[-1]].start)
    defect_go.start()
    defect_stay.start()

    later = tm > 1

    @pl.when(jnp.logical_not(later))
    def _():
        for z in order:
            hand_in(z)

    @pl.when(later)
    def _():
        queue = list(order)
        waiting = set(order)

        def leave(z):
            pl.when(has_next)(passed[z].start)
            hand_in(z)

        for index, z in enumerate(order):
            while waiting & {z - 1, z, z + 1}:
                come = queue.pop(0)
                waiting.remove(come)
                passed[come].wait_recv()
                if come == low_edge:
                    pl.when(has_low)(passed_low.start)
                if come == high_edge:
                    pl.when(has_high)(passed_high.start)
            if z == low_edge:
                pl.when(has_low)(passed_high.wait_recv)
            if z == high_edge:
                pl.when(has_high)(passed_low.wait_recv)
            middle, delta = change(before, z)
            after[z] = middle + coarse_ratio * delta + offset[z]
            if index:
                leave(order[index - 1])
        leave(order[-1])
        pl.when(has_low)(passed_low.wait_send)
        pl.when(has_high)(passed_high.wait_send)

    onward = jnp.logical_and(tm > 0, has_next)

    @pl.when(is_last)
    def _():
        for copy in initial_mate:
            copy.wait_send()

    @pl.when(has_next)
    def _():
        guess_own.wait_send()
        for copy in guess_mate:
            copy.wait_send()

    rate_mate.wait_send()
    twin_mate.wait_send()
    pl.when(has_high)(twin_low.wait_send)
    pl.when(has_low)(twin_high.wait_send)
    pl.when(has_low)(rate_low.wait_send)
    pl.when(has_high)(rate_high.wait_send)
    pl.when(own_low)(start_low.wait_send)
    pl.when(own_high)(start_high.wait_send)

    @pl.when(other_low)
    def _():
        for low, high in start_edges:
            low.wait_send()

    @pl.when(other_high)
    def _():
        for low, high in start_edges:
            high.wait_send()

    @pl.when(has_next)
    def _():
        for piece in range(PIECES):
            given[piece].wait_send()

    @pl.when(has_previous)
    def _():
        for piece in range(PIECES):
            pl.when(has_low)(given_low[piece].wait_send)
            pl.when(has_high)(given_high[piece].wait_send)

    @pl.when(onward)
    def _():
        for z in order:
            passed[z].wait_send()

    defect_stay.wait()
    defect_go.wait()
    for z in order:
        pl.when(at_home(z))(stay[z].wait)
        pl.when(at_home(z))(go[z].wait_recv)
        pl.when(jnp.logical_not(at_home(z)))(go[z].wait_send)


def on_device(nt, ns, initial, coarse_guess, react_rate):
    planes, across, width = initial.shape
    half = across // 2
    wide = -(-(2 * STEPS + max(nt - 2, 0)) // SUBLANES) * SUBLANES
    length = 2 * planes + 2 * STEPS
    field = pltpu.VMEM((length, half + 2 * wide, width), jnp.float32)
    slot_of, total = slots(planes)
    shape = jax.ShapeDtypeStruct(initial.shape, jnp.float32)
    corrected, defect = pl.pallas_call(
        functools.partial(kernel, nt, ns, planes, half, wide, slot_of),
        out_shape=(shape, shape),
        in_specs=[pl.BlockSpec(memory_space=pl.ANY)] * 3,
        out_specs=[pl.BlockSpec(memory_space=pl.ANY)] * 2,
        scratch_shapes=[field] * 11
        + [
            pltpu.VMEM((half + 2 * wide, width), jnp.float32),
            pltpu.SemaphoreType.DMA((total,)),
            pltpu.SemaphoreType.DMA((total,)),
            pltpu.SemaphoreType.DMA((3 + planes,)),
        ],
        compiler_params=pltpu.CompilerParams(collective_id=0, has_side_effects=True),
    )(initial, coarse_guess[0], react_rate)
    return corrected[None], defect[None]


def solution(mesh):
    in_specs = (P("space", None, None), P("tm", "space", None, None), P("space", None, None))
    out_specs = (P("tm", "space", None, None), P("tm", "space", None, None))
    return jax.shard_map(
        functools.partial(on_device, mesh.shape["tm"], mesh.shape["space"]),
        mesh=mesh, in_specs=in_specs, out_specs=out_specs, check_vma=False,
    )
```

```python
import functools

import jax
import jax.numpy as jnp
from jax import lax
from jax.experimental import pallas as pl
from jax.experimental.pallas import tpu as pltpu
from jax.sharding import PartitionSpec as P

STEPS = 3
SUBLANES = 8

fine_diffuse = 0.04
fine_growth = 0.05
coarse_ratio = 4.0

MESH = pl.DeviceIdType.MESH

PIECES = 4


def slots(planes):
    kinds = dict(
        start=2 + PIECES, start_edge=1 + PIECES, rate=1, rate_edge=2, rate_core=3, again=PIECES, again_edge=2 * PIECES,
        chain=2 * planes, chain_edge=2, defect=1, corrected=planes,
    )
    first, total = {}, 0
    for kind, number in kinds.items():
        first[kind] = total
        total += number
    return first, total


def kernel(
    nt, ns, planes, half, wide, slot_of,
    initial, guess, rate_in, corrected_out, defect_out,
    start, rate, again, before, first, second, relaxed, coarse, offset, defect, after, reach,
    send, recv, local,
):
    tm, space = lax.axis_index("tm"), lax.axis_index("space")
    pair, side = lax.div(space, 2), lax.rem(space, 2)
    pairs = ns // 2
    mate = space + 1 - 2 * side
    block = 2 * planes
    length = block + 2 * STEPS
    rows = half + 2 * wide
    has_low, has_high = pair > 0, pair < pairs - 1
    has_next, has_previous = tm < nt - 1, tm > 0
    own = pl.ds(STEPS, block)

    for ref in (start, rate, again, before):
        zero_plane = jnp.zeros((STEPS,) + ref.shape[1:], jnp.float32)
        zero_rows = jnp.zeros((block, wide, ref.shape[2]), jnp.float32)
        ref[0:STEPS] = zero_plane
        ref[STEPS + block : length] = zero_plane
        ref[STEPS : STEPS + block, 0:wide] = zero_rows
        ref[STEPS : STEPS + block, wide + half : rows] = zero_rows

    barrier = pltpu.get_barrier_semaphore()
    count = jnp.int32(0)
    for step in (-1, 0, 1):
        for place in ("own", "mate", "low", "high"):
            if step == 0 and place == "own":
                continue
            there = {"own": space, "mate": mate, "low": space - 2, "high": space + 2}[place]
            tests = []
            if step:
                tests.append(has_next if step > 0 else has_previous)
            if place in ("low", "high"):
                tests.append(has_low if place == "low" else has_high)
            target = {"tm": tm + step, "space": there}
            if tests:
                valid = functools.reduce(jnp.logical_and, tests)

                @pl.when(valid)
                def _(target=target):
                    pl.semaphore_signal(barrier, inc=1, device_id=target, device_id_type=MESH)

                count = count + valid.astype(jnp.int32)
            else:
                pl.semaphore_signal(barrier, inc=1, device_id=target, device_id_type=MESH)
                count = count + 1
    for here, there in ((tm == 0, nt - 1), (tm == nt - 1, 0)):

        @pl.when(here)
        def _(there=there):
            pl.semaphore_signal(
                barrier, inc=1, device_id={"tm": there, "space": mate}, device_id_type=MESH
            )

        count = count + here.astype(jnp.int32)
    pl.semaphore_wait(barrier, count)

    def remote(src, dst, slot, to_tm, to_space):
        return pltpu.make_async_remote_copy(
            src_ref=src,
            dst_ref=dst,
            send_sem=send.at[slot],
            recv_sem=recv.at[slot],
            device_id={"tm": to_tm, "space": to_space},
            device_id_type=MESH,
        )

    def cut(ref, target):
        return ref.at[:, pl.ds(pl.multiple_of(target * (half - wide), SUBLANES), half + wide), :]

    def spot(ref, target, begin, size):
        at = pl.multiple_of(wide * (1 - target), SUBLANES)
        return ref.at[pl.ds(begin, size), pl.ds(at, half + wide), :]

    slab = STEPS + planes * side
    other = STEPS + planes * (1 - side)

    core = lax.rem(tm, 2)
    twin = tm + 1 - 2 * core
    lanes = start.shape[2] // 2

    def lane_half(ref, which):
        return ref.at[:, :, pl.ds(pl.multiple_of(which * lanes, lanes), lanes)]

    groups = (half + wide) // SUBLANES
    bounds = [groups * piece // PIECES * SUBLANES for piece in range(PIECES + 1)]

    def piece_of(ref, begin, size, piece, target=side):
        at = pl.multiple_of(wide * (1 - target) + bounds[piece], SUBLANES)
        return ref.at[pl.ds(begin, size), pl.ds(at, bounds[piece + 1] - bounds[piece]), :]

    def cut_piece(ref, target, piece):
        at = pl.multiple_of(target * (half - wide) + bounds[piece], SUBLANES)
        return ref.at[:, pl.ds(at, bounds[piece + 1] - bounds[piece]), :]

    rate_own = pltpu.make_async_copy(cut(rate_in, side), spot(rate, side, slab, planes), local.at[0])
    rate_mate = remote(
        lane_half(cut(rate_in, 1 - side), core),
        lane_half(spot(rate, 1 - side, slab, planes), core),
        slot_of["rate"],
        tm,
        mate,
    )
    initial_own = pltpu.make_async_copy(cut(initial, side), spot(start, side, slab, planes), local.at[1])
    guess_own = remote(
        cut(guess, side), spot(start, side, slab, planes), slot_of["start"], tm + 1, space
    )

    def to_mate(ref, to_tm):
        return [
            remote(
                cut_piece(ref, 1 - side, piece),
                piece_of(start, slab, planes, piece, 1 - side),
                slot_of["start"] + 1 + piece,
                to_tm,
                mate,
            )
            for piece in range(PIECES)
        ]

    guess_mate = to_mate(guess, tm + 1)
    initial_mate = to_mate(initial, 0)
    is_last = tm == nt - 1

    rate_mate.start()
    rate_own.start()

    @pl.when(has_next)
    def _():
        guess_own.start()
        for copy in guess_mate:
            copy.start()

    @pl.when(is_last)
    def _():
        for copy in initial_mate:
            copy.start()

    @pl.when(tm == 0)
    def _():
        initial_own.start()

    for ref in (first, second):
        @pl.when(jnp.logical_not(has_low))
        def _(ref=ref):
            ref[0:STEPS] = jnp.zeros((STEPS,) + ref.shape[1:], jnp.float32)

        @pl.when(jnp.logical_not(has_high))
        def _(ref=ref):
            ref[STEPS + block : length] = jnp.zeros((STEPS,) + ref.shape[1:], jnp.float32)

    row = lax.broadcasted_iota(jnp.int32, reach.shape, 0)
    outside = jnp.logical_or(
        jnp.logical_and(side == 0, row < wide), jnp.logical_and(side == 1, row >= wide + half)
    )
    reach[...] = jnp.where(outside, 0.0, fine_diffuse)

    low_place, high_place = STEPS + block, 0

    def edge_pieces(piece):
        slot = slot_of["start_edge"] + 1 + piece
        low = remote(
            piece_of(start, STEPS, STEPS, piece), piece_of(start, low_place, STEPS, piece),
            slot, tm, space - 2,
        )
        high = remote(
            piece_of(start, block, STEPS, piece), piece_of(start, high_place, STEPS, piece),
            slot, tm, space + 2,
        )
        return low, high

    start_edges = [edge_pieces(piece) for piece in range(PIECES)]
    start_low = remote(
        spot(start, side, STEPS, STEPS), spot(start, side, low_place, STEPS),
        slot_of["start_edge"], tm, space - 2,
    )
    start_high = remote(
        spot(start, side, block, STEPS), spot(start, side, high_place, STEPS),
        slot_of["start_edge"], tm, space + 2,
    )
    reach_rate = STEPS - 1
    rate_low_spot = lane_half(spot(rate, side, low_place, reach_rate), core)
    rate_high_spot = lane_half(spot(rate, side, high_place + 1, reach_rate), core)
    rate_low = remote(
        lane_half(spot(rate, side, STEPS, reach_rate), core), rate_low_spot,
        slot_of["rate_edge"], tm, space - 2,
    )
    rate_high = remote(
        lane_half(spot(rate, side, STEPS + block - reach_rate, reach_rate), core), rate_high_spot,
        slot_of["rate_edge"] + 1, tm, space + 2,
    )
    rate_other_spot = lane_half(spot(rate, side, other, planes), core)
    twin_mate = remote(rate_other_spot, rate_other_spot, slot_of["rate_core"], twin, space)
    twin_low = remote(rate_low_spot, rate_low_spot, slot_of["rate_core"] + 1, twin, space)
    twin_high = remote(rate_high_spot, rate_high_spot, slot_of["rate_core"] + 2, twin, space)

    own_low = jnp.logical_and(side == 0, has_low)
    own_high = jnp.logical_and(side == 1, has_high)
    other_low = jnp.logical_and(side == 1, has_low)
    other_high = jnp.logical_and(side == 0, has_high)

    rate_own.wait()
    pl.when(own_low)(rate_low.start)
    pl.when(own_high)(rate_high.start)

    @pl.when(tm == 0)
    def _():
        initial_own.wait()

    @pl.when(has_previous)
    def _():
        guess_own.wait_recv()

    pl.when(own_low)(start_low.start)
    pl.when(own_high)(start_high.start)

    rate_mate.wait_recv()
    pl.when(other_low)(rate_low.start)
    pl.when(other_high)(rate_high.start)
    twin_mate.start()

    for piece in range(PIECES):
        guess_mate[piece].wait_recv()
        pl.when(other_low)(start_edges[piece][0].start)
        pl.when(other_high)(start_edges[piece][1].start)

    @pl.when(has_high)
    def _():
        rate_low.wait_recv()
        twin_low.start()

    @pl.when(has_low)
    def _():
        rate_high.wait_recv()
        twin_high.start()

    twin_mate.wait_recv()
    pl.when(has_high)(twin_low.wait_recv)
    pl.when(has_low)(twin_high.wait_recv)

    @pl.when(jnp.logical_and(side == 0, has_high))
    def _():
        start_low.wait_recv()

    @pl.when(jnp.logical_and(side == 1, has_low))
    def _():
        start_high.wait_recv()

    @pl.when(jnp.logical_and(side == 1, has_high))
    def _():
        for low, high in start_edges:
            low.wait_recv()

    @pl.when(jnp.logical_and(side == 0, has_low))
    def _():
        for low, high in start_edges:
            high.wait_recv()

    keep = pltpu.make_async_copy(start, again, local.at[1])

    @pl.when(tm == 0)
    def _():
        keep.start()

    width = start.shape[2]
    lane = lax.broadcasted_iota(jnp.int32, reach.shape, 1)

    def change(ref, z):
        middle = ref[z]
        beside = ref[z + 1] + ref[z - 1]
        beside = beside + pltpu.roll(middle, 1, 0) + pltpu.roll(middle, rows - 1, 0)
        beside = beside + jnp.where(lane == 0, 0.0, pltpu.roll(middle, 1, 1))
        beside = beside + jnp.where(lane == width - 1, 0.0, pltpu.roll(middle, width - 1, 1))
        growth = rate[z] * (fine_growth - fine_growth * (middle * middle))
        return middle, reach[...] * beside + middle * (growth - 6.0 * fine_diffuse)

    def span(step):
        low = jnp.where(has_low, step, max(step, STEPS))
        high = jnp.where(has_high, length - step, min(length - step, STEPS + block))
        return low, high

    def fine(src, dst, step):
        def plane(z, carry):
            middle, delta = change(src, z)
            dst[z] = middle + delta
            return carry

        lax.fori_loop(*span(step), plane, 0)

    fine(start, first, 1)
    fine(first, second, 2)
    fine(second, relaxed, 3)

    given, given_low, given_high = [], [], []
    for piece in range(PIECES):
        slot = slot_of["again_edge"] + 2 * piece
        given.append(
            remote(
                piece_of(relaxed, STEPS, block, piece),
                piece_of(again, STEPS, block, piece),
                slot_of["again"] + piece,
                tm + 1,
                space,
            )
        )
        given_low.append(
            remote(
                piece_of(again, STEPS, STEPS, piece),
                piece_of(again, STEPS + block, STEPS, piece),
                slot,
                tm,
                space - 2,
            )
        )
        given_high.append(
            remote(
                piece_of(again, block, STEPS, piece),
                piece_of(again, 0, STEPS, piece),
                slot + 1,
                tm,
                space + 2,
            )
        )

    @pl.when(has_next)
    def _():
        for piece in range(PIECES):
            given[piece].start()

    @pl.when(tm == 0)
    def _():
        keep.wait()

    @pl.when(has_previous)
    def _():
        for piece in range(PIECES):
            given[piece].wait_recv()
            pl.when(has_low)(given_low[piece].start)
            pl.when(has_high)(given_high[piece].start)
        for piece in range(PIECES):
            pl.when(has_high)(given_low[piece].wait_recv)
            pl.when(has_low)(given_high[piece].wait_recv)

    def first_plane(z, carry):
        middle, delta = change(again, z)
        first[z] = middle + delta
        coarse[z] = middle + coarse_ratio * delta
        return carry

    lax.fori_loop(*span(1), first_plane, 0)
    fine(first, second, 2)

    order = []
    for depth in range(planes):
        order += [STEPS + depth, STEPS + block - 1 - depth]

    def row_span(z):
        at = pl.multiple_of(wide * (1 - side), SUBLANES)
        return (pl.ds(z, 1), pl.ds(at, half + wide), slice(None))

    passed = {
        z: remote(
            after.at[row_span(z)], before.at[row_span(z)], slot_of["chain"] + z - STEPS, tm + 1, space
        )
        for z in order
    }
    low_edge, high_edge = STEPS, STEPS + block - 1
    passed_low = remote(
        before.at[row_span(low_edge)], before.at[row_span(high_edge + 1)],
        slot_of["chain_edge"], tm, space - 2,
    )
    passed_high = remote(
        before.at[row_span(high_edge)], before.at[row_span(low_edge - 1)],
        slot_of["chain_edge"] + 1, tm, space + 2,
    )

    mine = pl.ds(pl.multiple_of(side * half, SUBLANES), half)
    middle_rows = pl.ds(wide, half)
    defect_stay = pltpu.make_async_copy(
        defect.at[pl.ds(slab, planes), middle_rows, :], defect_out.at[:, mine, :], local.at[2]
    )
    defect_go = remote(
        defect.at[pl.ds(other, planes), middle_rows, :], defect_out.at[:, mine, :],
        slot_of["defect"], tm, mate,
    )
    stay, go = {}, {}
    for z in order:
        place = (z - STEPS) % planes
        src = after.at[pl.ds(z, 1), middle_rows, :]
        dst = corrected_out.at[pl.ds(place, 1), mine, :]
        stay[z] = pltpu.make_async_copy(src, dst, local.at[3 + place])
        go[z] = remote(src, dst, slot_of["corrected"] + place, tm, mate)

    def at_home(z):
        return side == (z - STEPS) // planes

    def hand_in(z):
        pl.when(at_home(z))(stay[z].start)
        pl.when(jnp.logical_not(at_home(z)))(go[z].start)

    def last_plane(z):
        middle, delta = change(second, z)
        end = middle + delta
        defect[z] = end - relaxed[z]
        shift = end - coarse[z]
        offset[z] = shift
        after[z] = coarse[z] + shift

    def take_edges():
        passed[low_edge].wait_recv()
        pl.when(has_low)(passed_low.start)
        passed[high_edge].wait_recv()
        pl.when(has_high)(passed_high.start)

    pl.when(tm == 2)(take_edges)
    opens = jnp.logical_and(tm == 1, has_next)
    for index, z in enumerate(order):
        last_plane(z)
        if index:
            pl.when(opens)(passed[order[index - 1]].start)
    pl.when(opens)(passed[order[-1]].start)
    defect_go.start()
    defect_stay.start()

    later = tm > 1

    @pl.when(jnp.logical_not(later))
    def _():
        for z in order:
            hand_in(z)

    @pl.when(later)
    def _():
        pl.when(tm > 2)(take_edges)
        queue = order[2:]
        waiting = set(queue)

        def leave(z):
            pl.when(has_next)(passed[z].start)
            hand_in(z)

        for index, z in enumerate(order):
            while waiting & {z - 1, z, z + 1}:
                come = queue.pop(0)
                waiting.remove(come)
                passed[come].wait_recv()
            if z == low_edge:
                pl.when(has_low)(passed_high.wait_recv)
            if z == high_edge:
                pl.when(has_high)(passed_low.wait_recv)
            middle, delta = change(before, z)
            after[z] = middle + coarse_ratio * delta + offset[z]
            if index:
                leave(order[index - 1])
        leave(order[-1])
        pl.when(has_low)(passed_low.wait_send)
        pl.when(has_high)(passed_high.wait_send)

    onward = jnp.logical_and(tm > 0, has_next)

    @pl.when(is_last)
    def _():
        for copy in initial_mate:
            copy.wait_send()

    @pl.when(has_next)
    def _():
        guess_own.wait_send()
        for copy in guess_mate:
            copy.wait_send()

    rate_mate.wait_send()
    twin_mate.wait_send()
    pl.when(has_high)(twin_low.wait_send)
    pl.when(has_low)(twin_high.wait_send)
    pl.when(has_low)(rate_low.wait_send)
    pl.when(has_high)(rate_high.wait_send)
    pl.when(own_low)(start_low.wait_send)
    pl.when(own_high)(start_high.wait_send)

    @pl.when(other_low)
    def _():
        for low, high in start_edges:
            low.wait_send()

    @pl.when(other_high)
    def _():
        for low, high in start_edges:
            high.wait_send()

    @pl.when(has_next)
    def _():
        for piece in range(PIECES):
            given[piece].wait_send()

    @pl.when(has_previous)
    def _():
        for piece in range(PIECES):
            pl.when(has_low)(given_low[piece].wait_send)
            pl.when(has_high)(given_high[piece].wait_send)

    @pl.when(onward)
    def _():
        for z in order:
            passed[z].wait_send()

    defect_stay.wait()
    defect_go.wait()
    for z in order:
        pl.when(at_home(z))(stay[z].wait)
        pl.when(at_home(z))(go[z].wait_recv)
        pl.when(jnp.logical_not(at_home(z)))(go[z].wait_send)


def on_device(nt, ns, initial, coarse_guess, react_rate):
    planes, across, width = initial.shape
    half = across // 2
    wide = -(-(2 * STEPS + max(nt - 2, 0)) // SUBLANES) * SUBLANES
    length = 2 * planes + 2 * STEPS
    field = pltpu.VMEM((length, half + 2 * wide, width), jnp.float32)
    slot_of, total = slots(planes)
    shape = jax.ShapeDtypeStruct(initial.shape, jnp.float32)
    corrected, defect = pl.pallas_call(
        functools.partial(kernel, nt, ns, planes, half, wide, slot_of),
        out_shape=(shape, shape),
        in_specs=[pl.BlockSpec(memory_space=pl.ANY)] * 3,
        out_specs=[pl.BlockSpec(memory_space=pl.ANY)] * 2,
        scratch_shapes=[field] * 11
        + [
            pltpu.VMEM((half + 2 * wide, width), jnp.float32),
            pltpu.SemaphoreType.DMA((total,)),
            pltpu.SemaphoreType.DMA((total,)),
            pltpu.SemaphoreType.DMA((3 + planes,)),
        ],
        compiler_params=pltpu.CompilerParams(collective_id=0, has_side_effects=True),
    )(initial, coarse_guess[0], react_rate)
    return corrected[None], defect[None]


def solution(mesh):
    in_specs = (P("space", None, None), P("tm", "space", None, None), P("space", None, None))
    out_specs = (P("tm", "space", None, None), P("tm", "space", None, None))
    return jax.shard_map(
        functools.partial(on_device, mesh.shape["tm"], mesh.shape["space"]),
        mesh=mesh, in_specs=in_specs, out_specs=out_specs, check_vma=False,
    )
```
